128 devices in a mesh: row: 8 (over y_lo, z), col: 16 (over y_hi, x, core).
Axes of the slice: x: 4, y: 4 (y_hi: 2, y_lo: 2; y = y_hi * 2 + y_lo), z: 4, core: 2. Of those that a mesh axis runs over, the one named last changes fastest.
Arguments:
- grad: bfloat16 [4096, 16384], P('row', 'col'), may hold values from -6 to 6
- first_moment: bfloat16 [4096, 16384], P('row', 'col'), may hold values from -6 to 6
- second_moment: bfloat16 [4096, 16384], P('row', 'col'), may hold values from 0.049804688 to 2
- left_basis: bfloat16 [4096, 4096], P(None, 'row'), may hold values from -0.09375 to 0.09375
- right_basis: bfloat16 [16384, 4096], P('col'), may hold values from -0.09375 to 0.09375
- left_eig: float32 [4096], P('row'), may hold values from 0.05 to 2
- right_eig: float32 [16384], P('col'), may hold values from 0.05 to 2
Outputs:
- first_new: bfloat16 [4096, 16384], P('row', 'col')
- second_new: bfloat16 [4096, 16384], P('row', 'col')
- update: bfloat16 [4096, 16384], P(('row', 'col'))
The draws below stay inside these ranges and needn't reach their ends.
All inputs are finite; a program needn't handle non-finite values.
Results may differ from the reference program's by a relative error of at most 0.014.
Values may be sent and summed in bfloat16 or wider, within the bound.
No kernel may reach another device: no remote copies, remote signals or barrier semaphores. Data moves between devices by JAX's collectives and lax.ppermute only.
A program may use at most 128 MiB of HBM per device.

```python
import math
import jax
import jax.numpy as jnp

D = 4096
F = 16384
BR = 4096


def level_of(stream_key, extent, pieces, least, top_value):
    def one(dim, blocks):
        draws = jax.random.uniform(jax.random.fold_in(jax.random.fold_in(stream_key, 6), dim), (blocks,), jnp.float32, least / len(pieces), top_value / len(pieces))
        return jnp.repeat(jnp.exp(draws), extent[dim] // blocks).reshape((-1,) + (1,) * (len(extent) - dim - 1))

    factor_of = one(*pieces[0])
    for cut in pieces[1:]:
        factor_of = factor_of * one(*cut)
    return factor_of


def scatter_about(own_key, shape, scale, most, cuts=(), held_as=jnp.bfloat16):
    entries = jax.random.normal(own_key, shape, jnp.float32) * scale
    if len(cuts) > 0:
        entries = level_of(own_key, shape, cuts, -0.22, 0.18) * entries
    return jnp.clip(entries, min=-most, max=most).astype(held_as)


def setup_inputs(seed: int = 0) -> dict:
    key_of = jax.random.split(jax.random.key(seed), 8)
    grad = scatter_about(key_of[0], (D, F), 1.0, 6.0, ((0, 8), (1, 16)))
    first_moment = scatter_about(key_of[1], (D, F), 1.0, 6.0, ((0, 8), (1, 16)))
    second_moment = jnp.clip(jnp.exp(math.log(2.0) - 3.6927934 * jax.random.uniform(key_of[2], (D, F), jnp.float32) ** level_of(key_of[2], (D, F), ((0, 8), (1, 16)), -0.2, 0.2)), 0.049804688, 2.0).astype(jnp.bfloat16)
    left_basis = scatter_about(key_of[3], (D, D), D ** -0.5, 0.09375, ((1, 8),))
    right_basis = scatter_about(key_of[4], (F, BR), BR ** -0.5, 0.09375, ((0, 16),))
    left_eig = jnp.clip(jnp.exp(math.log(2.0) - 3.6888794 * jax.random.uniform(key_of[5], (D,), jnp.float32) ** level_of(key_of[5], (D,), ((0, 8),), -0.2, 0.2)), 0.05, 2.0)
    right_eig = jnp.clip(jnp.exp(math.log(2.0) - 3.6888794 * jax.random.uniform(key_of[6], (F,), jnp.float32) ** level_of(key_of[6], (F,), ((0, 16),), -0.2, 0.2)), 0.05, 2.0)
    return dict(grad=grad, first_moment=first_moment, second_moment=second_moment, left_basis=left_basis, right_basis=right_basis, left_eig=left_eig, right_eig=right_eig)


def reference(grad, first_moment, second_moment, left_basis, right_basis, left_eig, right_eig):
    blocks = F // BR
    lefted = jnp.dot(left_basis.T, grad, preferred_element_type=jnp.float32).astype(jnp.bfloat16)
    right_three = right_basis.reshape(blocks, BR, BR).astype(jnp.float32)
    rotated = jnp.einsum('dkf,kbf->dkb', lefted.reshape(D, blocks, BR).astype(jnp.float32), right_three).reshape(D, F)
    first_full = 0.8 * first_moment.astype(jnp.float32) + 0.2 * rotated
    second_full = 0.9 * second_moment.astype(jnp.float32) + 0.1 * rotated * rotated
    damping = jnp.minimum(left_eig[:, None] * right_eig[None, :], 1.0)
    direction = (first_full / jnp.sqrt(second_full + damping)).astype(jnp.bfloat16)
    unrotated = jnp.einsum('dkb,kbf->dkf', direction.reshape(D, blocks, BR).astype(jnp.float32), right_three)
    unrotated = unrotated.reshape(D, F).astype(jnp.bfloat16)
    update = jnp.dot(left_basis, unrotated, preferred_element_type=jnp.float32).astype(jnp.bfloat16)
    return (first_full.astype(jnp.bfloat16), second_full.astype(jnp.bfloat16), update)
```

```python
import jax
import jax.numpy as jnp
from jax import lax
from jax.sharding import PartitionSpec as P

BF = jnp.bfloat16
F32 = jnp.float32
AXES = ("row", "col")
FWD_CUTS = (0, 2, 4)
BACK_CUTS = (0, 2, 4)


def linear(y, x, z, core):
    return ((y % 2) * 4 + z % 4) * 16 + (y % 4 // 2) * 8 + (x % 4) * 2 + core


def pairs_of(move):
    return [
        (linear(y, x, z, core), linear(*move(y, x, z, core)))
        for y in range(4)
        for x in range(4)
        for z in range(4)
        for core in range(2)
    ]


MOVES = {
    "z+": pairs_of(lambda y, x, z, c: (y, x, z + 1, c)),
    "z-": pairs_of(lambda y, x, z, c: (y, x, z - 1, c)),
    "yp": pairs_of(lambda y, x, z, c: (y ^ 1, x, z, c)),
    "yc": pairs_of(lambda y, x, z, c: (y + 1 if y % 2 else y - 1, x, z, c)),
    "y+": pairs_of(lambda y, x, z, c: (y + 1, x, z, c)),
    "y-": pairs_of(lambda y, x, z, c: (y - 1, x, z, c)),
    "y2": pairs_of(lambda y, x, z, c: (y + 2, x, z, c)),
    "xp": pairs_of(lambda y, x, z, c: (y, x ^ 1, z, c)),
    "x+": pairs_of(lambda y, x, z, c: (y, x + 1, z, c)),
    "x-": pairs_of(lambda y, x, z, c: (y, x - 1, z, c)),
    "x2": pairs_of(lambda y, x, z, c: (y, x + 2, z, c)),
    "co": pairs_of(lambda y, x, z, c: (y, x, z, 1 - c)),
}


def move(value, name):
    return lax.ppermute(value, AXES, MOVES[name])


def dot(a, b, contract):
    return lax.dot_general(a, b, ((contract[:1], contract[1:]), ((), ())), preferred_element_type=F32)


def per_device(grad, first_moment, second_moment, left_basis, right_basis, left_eig, right_eig):
    rows, cols = grad.shape
    half = cols // 2
    unit = half // 4
    row, col = lax.axis_index("row"), lax.axis_index("col")
    y_lo, z = row // 4, row % 4
    y_hi, x, core = col // 8, col // 2 % 4, col % 2
    x_lo = x % 2
    y = y_hi * 2 + y_lo
    quarter = left_basis.shape[0] // 2

    mine = lax.dynamic_slice_in_dim(left_basis, core * quarter, quarter, 0)
    cut = quarter * 3 // 8
    part_a = move(mine[:cut], "yp")
    part_b = move(mine[cut:], "yc")
    fetched = jnp.concatenate([part_a, part_b], 0)
    fetched_other = jnp.concatenate([move(part_a, "co"), move(part_b, "co")], 0)

    def rolled(upper, lower):
        own = jnp.where(y_lo == 0, upper, lower)
        other = jnp.where(y_lo == 0, lower, upper)
        out = []
        for j in range(4):
            at = (z + j) % 4 * rows
            out.append(
                jnp.concatenate(
                    [
                        lax.dynamic_slice_in_dim(own, at, rows, 0),
                        lax.dynamic_slice_in_dim(other, at, rows, 0),
                    ],
                    0,
                )
            )
        return out

    left_own = []
    for j in range(4):
        at = (z + j) % 4 * rows
        left_own.append(
            jnp.concatenate(
                [
                    lax.dynamic_slice_in_dim(left_basis, y_lo * quarter + at, rows, 0),
                    lax.dynamic_slice_in_dim(left_basis, (1 - y_lo) * quarter + at, rows, 0),
                ],
                0,
            )
        )
    left_part = rolled(
        jnp.where(core == 0, fetched, fetched_other), jnp.where(core == 0, fetched_other, fetched)
    )

    def right_part(core_rel, lo, hi):
        pieces = []
        for x_rel in range(2):
            for y_rel in range(2):
                at = ((x_lo ^ x_rel) * 2 + (core ^ core_rel)) * cols + (y_lo ^ y_rel) * half + lo
                pieces.append(lax.dynamic_slice_in_dim(right_basis, at, hi - lo, 1))
        return jnp.concatenate(pieces, 1)

    keep = lax.dynamic_slice_in_dim(grad, y_lo * half, half, 1)
    give = lax.dynamic_slice_in_dim(grad, (1 - y_lo) * half, half, 1)
    rotated = None
    for lo, hi in zip(FWD_CUTS[:-1], FWD_CUTS[1:]):
        lo, hi = lo * unit, hi * unit
        here = jnp.concatenate([keep[:, lo:hi], move(give[:, lo:hi], "yp")], 0)
        below, above = move(here, "z+"), move(here, "z-")
        far_top, far_bottom = move(above[:rows], "z-"), move(below[rows:], "z+")
        blocks = (here, above, jnp.concatenate([far_top, far_bottom], 0), below)

        def lefted(left):
            total = None
            for j in (0, 1, 3, 2):
                term = dot(left[j], blocks[j], (0, 0))
                total = term if total is None else total + term
            return total.astype(BF)

        part = move(lefted(left_part), "yp")
        own = lefted(left_own)
        ours = jnp.concatenate([own, part, move(own, "xp"), move(part, "xp")], 1)
        term = dot(ours, right_part(0, lo, hi), (1, 1))
        rotated = term if rotated is None else rotated + term
        rotated = rotated + dot(move(ours, "co"), right_part(1, lo, hi), (1, 1))

    first_full = 0.8 * first_moment.astype(F32) + 0.2 * rotated
    second_full = 0.9 * second_moment.astype(F32) + 0.1 * rotated * rotated
    damping = jnp.minimum(left_eig[:, None] * right_eig[None, :], 1.0)
    direction = (first_full / jnp.sqrt(second_full + damping)).astype(BF)

    done = []
    for lo, hi in zip(BACK_CUTS[:-1], BACK_CUTS[1:]):
        lo, hi = lo * unit, hi * unit
        w = hi - lo
        sent = move(dot(direction, right_part(1, lo, hi), (1, 0)).astype(BF), "co")
        sums = dot(direction, right_part(0, lo, hi), (1, 0)) + sent.astype(F32)
        arrived = move(sums[:, 2 * w :].astype(BF), "xp")
        unrotated = (sums[:, : 2 * w] + arrived.astype(F32)).astype(BF)
        own = unrotated[:, :w]
        part = move(unrotated[:, w:], "yp")

        def product(j):
            return dot(left_own[j], own, (1, 0)) + dot(left_part[j], part, (1, 0))

        far = product(2).astype(BF)
        top, bottom = move(far[:rows], "z+"), move(far[rows:], "z-")
        p1, p3 = product(1), product(3)
        p1 = jnp.concatenate([p1[:rows] + top.astype(F32), p1[rows:]], 0).astype(BF)
        p3 = jnp.concatenate([p3[:rows], p3[rows:] + bottom.astype(F32)], 0).astype(BF)
        total = product(0) + move(p1, "z+").astype(F32) + move(p3, "z-").astype(F32)
        total = total.astype(BF)

        cell = rows // 16
        total = total.reshape(2, 2, 4, 2, cell, w)
        stay = lax.dynamic_index_in_dim(total, core, 3, keepdims=False)
        go = move(lax.dynamic_index_in_dim(total, 1 - core, 3, keepdims=False), "co")
        both = jnp.where(core == 0, jnp.stack([stay, go], 3), jnp.stack([go, stay], 3))

        def to_y(rel):
            dest = (y + rel) % 4
            return lax.dynamic_index_in_dim(both[rel % 2], dest // 2, 0, keepdims=False)

        by_y = {0: to_y(0), 3: move(to_y(1), "y+"), 1: move(to_y(3), "y-"), 2: move(to_y(2), "y2")}
        stacked = jnp.stack([by_y[r] for r in range(4)], 0)
        stacked = jnp.take(stacked, (jnp.arange(4) - y) % 4, axis=0)

        def to_x(rel):
            return lax.dynamic_index_in_dim(stacked, (x + rel) % 4, 1, keepdims=False)

        by_x = {0: to_x(0), 3: move(to_x(1), "x+"), 1: move(to_x(3), "x-"), 2: move(to_x(2), "x2")}
        final = jnp.stack([by_x[r] for r in range(4)], 0)
        final = jnp.take(final, (jnp.arange(4) - x) % 4, axis=0)
        done.append(final)
    update = jnp.concatenate(done, -1)
    cell = update.shape[3]
    update = update.reshape(4, 2, 2, 2, cell, half).transpose(4, 1, 0, 3, 2, 5)
    update = update.reshape(cell, -1)
    return (first_full.astype(BF), second_full.astype(BF), update)


def solution(mesh):
    placed = (
        P("row", "col"),
        P("row", "col"),
        P("row", "col"),
        P(None, "row"),
        P("col", None),
        P("row"),
        P("col"),
    )
    return jax.shard_map(
        per_device,
        mesh=mesh,
        in_specs=placed,
        out_specs=(P("row", "col"), P("row", "col"), P(("row", "col"), None)),
        check_vma=False,
    )
```

```python
import functools
import math

import jax
import jax.numpy as jnp
from jax import lax
from jax.experimental import pallas as pl
from jax.experimental.pallas import tpu as pltpu
from jax.sharding import PartitionSpec as P


BF = jnp.bfloat16
F32 = jnp.float32
AXES = ("row", "col")
CUTS = (0, 2, 4)


def linear(y, x, z, core):
    return ((y % 2) * 4 + z % 4) * 16 + (y % 4 // 2) * 8 + (x % 4) * 2 + core


def pairs_of(move):
    return [
        (linear(y, x, z, core), linear(*move(y, x, z, core)))
        for y in range(4)
        for x in range(4)
        for z in range(4)
        for core in range(2)
    ]


MOVES = {
    "z+": pairs_of(lambda y, x, z, c: (y, x, z + 1, c)),
    "z-": pairs_of(lambda y, x, z, c: (y, x, z - 1, c)),
    "yp": pairs_of(lambda y, x, z, c: (y ^ 1, x, z, c)),
    "yc": pairs_of(lambda y, x, z, c: (y + 1 if y % 2 else y - 1, x, z, c)),
    "y+": pairs_of(lambda y, x, z, c: (y + 1, x, z, c)),
    "y-": pairs_of(lambda y, x, z, c: (y - 1, x, z, c)),
    "y2": pairs_of(lambda y, x, z, c: (y + 2, x, z, c)),
    "xp": pairs_of(lambda y, x, z, c: (y, x ^ 1, z, c)),
    "x+": pairs_of(lambda y, x, z, c: (y, x + 1, z, c)),
    "x-": pairs_of(lambda y, x, z, c: (y, x - 1, z, c)),
    "x2": pairs_of(lambda y, x, z, c: (y, x + 2, z, c)),
    "co": pairs_of(lambda y, x, z, c: (y, x, z, 1 - c)),
}


def move(value, name):
    return lax.ppermute(value, AXES, MOVES[name])


def dot(a, b, contract):
    return lax.dot_general(a, b, ((contract[:1], contract[1:]), ((), ())), preferred_element_type=F32)


def call(kernel, shapes, spot, *operands):
    several = isinstance(shapes, list)
    outs = shapes if several else [jax.ShapeDtypeStruct(shapes, BF)]
    moved = sum(v.size * v.dtype.itemsize for v in operands) + sum(
        math.prod(v.shape) * v.dtype.itemsize for v in outs
    )
    return pl.pallas_call(
        kernel,
        out_shape=outs if several else outs[0],
        in_specs=[pl.BlockSpec(memory_space=pltpu.SMEM)]
        + [pl.BlockSpec(memory_space=pltpu.VMEM)] * len(operands),
        out_specs=[pl.BlockSpec(memory_space=pltpu.VMEM)] * len(outs)
        if several
        else pl.BlockSpec(memory_space=pltpu.VMEM),
        compiler_params=pltpu.CompilerParams(vmem_limit_bytes=moved + 2**20),
        cost_estimate=pl.CostEstimate(flops=0, bytes_accessed=moved, transcendentals=0),
    )(spot, *operands)


def copy_rows(source, source_at, target, target_at, rows):
    slab = math.gcd(rows, 128)

    def body(n, carry):
        take = pl.ds(pl.multiple_of(source_at + n * slab, slab), slab)
        put = pl.ds(pl.multiple_of(target_at + n * slab, slab), slab)
        target[put, :] = source[take, :].astype(target.dtype)
        return carry

    lax.fori_loop(0, rows // slab, body, 0)


def split_kernel(order, spot_ref, product, *outs):
    z, y_lo = spot_ref[0], spot_ref[1]
    rows = outs[0].shape[0] // 2
    for j, out in zip(order, outs):
        for rel in range(2):
            at = ((y_lo + rel) % 2 * 4 + (z + j) % 4) * rows
            copy_rows(product, at, out, rel * rows, rows)


def stack_kernel(spot_ref, here, below, above, far, out_ref):
    z, y_lo = spot_ref[0], spot_ref[1]
    rows = here.shape[0] // 2
    for j, piece in ((0, here), (3, below), (1, above), (2, far)):
        for rel in range(2):
            at = ((y_lo + rel) % 2 * 4 + (z + j) % 4) * rows
            copy_rows(piece, rel * rows, out_ref, at, rows)


def sum_kernel(spot_ref, here, first, last, stay, go):
    core = spot_ref[2]
    cells, cell = stay.shape[0], stay.shape[1]

    def body(n, carry):
        for out, which in ((stay, core), (go, 1 - core)):
            at = pl.ds(pl.multiple_of((2 * n + which) * cell, cell), cell)
            out[n] = (here[at, :] + first[at, :].astype(F32) + last[at, :].astype(F32)).astype(BF)
        return carry

    lax.fori_loop(0, cells, body, 0)


def pack_y_kernel(spot_ref, stay, come, *outs):
    y = spot_ref[4]
    for rel, out in zip((0, 3, 2, 1), outs):
        at = rel % 2 * 8 + (y + rel) % 4 // 2 * 4
        for c, piece in enumerate((stay, come)):
            out[c] = piece[pl.ds(at, 4)]


def pack_x_kernel(spot_ref, *refs):
    x = spot_ref[3]
    pieces, outs = refs[:-4], refs[-4:]
    for rel, out in zip((0, 3, 2, 1), outs):
        at = (x + rel) % 4
        for r, piece in enumerate(pieces):
            for c in range(2):
                out[r, c] = piece[c, at]


def blocks_kernel(spot_ref, *refs):
    *pieces, out_ref = refs
    core = spot_ref[2]
    total = out_ref.shape[0] // 2
    for n, piece in enumerate(pieces):
        at = (core + n // 2) % 2 * total + n % 2 * pieces[0].shape[0]
        copy_rows(piece, 0, out_ref, at, piece.shape[0])


def roll_kernel(order_ref, in_0, in_1, out_0, out_1):
    copy_rows(in_0, 0, out_0, 0, in_0.shape[0])
    copy_rows(in_1, 0, out_1, 0, in_1.shape[0])


def place_kernel(cuts, spot_ref, *refs):
    *pieces, out_ref = refs
    x, y, core = spot_ref[3], spot_ref[4], spot_ref[2]
    half = out_ref.shape[1] // 32
    unit = half // 4
    for chunk, lo in enumerate(cuts[:-1]):
        w = (cuts[chunk + 1] - lo) * unit
        for x_rel in range(4):
            piece = pieces[chunk * 4 + x_rel]
            for y_rel in range(4):
                for core_rel in range(2):
                    from_y = (y + y_rel) % 4
                    slot = from_y // 2 * 16 + (x + x_rel) % 4 * 4 + (core + core_rel) % 2 * 2 + from_y % 2
                    at = pl.multiple_of(slot * half + lo * unit, unit)
                    out_ref[:, pl.ds(at, w)] = piece[y_rel, core_rel]


def step(grad, first_moment, second_moment, left_basis, right_basis, left_eig, right_eig):
    rows, cols = grad.shape
    half = cols // 2
    unit = half // 4
    row, col = lax.axis_index("row"), lax.axis_index("col")
    y_lo, z = row // 4, row % 4
    y_hi, x, core = col // 8, col // 2 % 4, col % 2
    x_lo = x % 2
    y = y_hi * 2 + y_lo
    spot = jnp.stack([z, y_lo, core, x, y]).astype(jnp.int32)
    full = left_basis.shape[0]
    spans = [(lo * unit, hi * unit) for lo, hi in zip(CUTS[:-1], CUTS[1:])]

    keep = [lax.dynamic_slice_in_dim(grad, y_lo * half + lo, hi - lo, 1) for lo, hi in spans]
    give = [lax.dynamic_slice_in_dim(grad, (1 - y_lo) * half + lo, hi - lo, 1) for lo, hi in spans]
    given = [move(v, "yp") for v in give]

    block = full // 2 * 5 // 8
    block_c = move(lax.dynamic_slice_in_dim(left_basis, core * (full // 2), block, 0), "yc")
    block_p = move(
        lax.dynamic_slice_in_dim(left_basis, core * (full // 2) + block, full // 2 - block, 0), "yp"
    )
    other_c = move(block_c, "co")
    other_p = move(block_p, "co")
    left_part = call(
        blocks_kernel, left_basis.shape, spot, block_c, block_p, other_c, other_p
    )

    width = half // len(spans)
    right = []
    for i in range(len(spans)):
        slots = []
        for core_rel in range(2):
            for x_rel in range(2):
                for y_rel in range(2):
                    at = ((x_lo ^ x_rel) * 2 + (core ^ core_rel)) * 2 + (y_lo ^ y_rel)
                    slots.append(at * len(spans) + i)
        right += pl.pallas_call(
            roll_kernel,
            out_shape=[jax.ShapeDtypeStruct((right_basis.shape[0], 4 * width), BF)] * 2,
            grid_spec=pltpu.PrefetchScalarGridSpec(
                num_scalar_prefetch=1,
                grid=(4,),
                in_specs=[
                    pl.BlockSpec((right_basis.shape[0], width), lambda n, order: (0, order[n])),
                    pl.BlockSpec((right_basis.shape[0], width), lambda n, order: (0, order[n + 4])),
                ],
                out_specs=[pl.BlockSpec((right_basis.shape[0], width), lambda n, order: (0, n))] * 2,
            ),
            compiler_params=pltpu.CompilerParams(
                vmem_limit_bytes=right_basis.shape[0] * width * 16 + 2**20
            ),
            cost_estimate=pl.CostEstimate(
                flops=0, bytes_accessed=2 * right_basis.size, transcendentals=0
            ),
        )(jnp.stack(slots).astype(jnp.int32), right_basis, right_basis)

    rotated = None
    for i, (lo, hi) in enumerate(spans):
        here = jnp.concatenate([keep[i], given[i]], 0)
        below, above = move(here, "z+"), move(here, "z-")
        far = move(above, "z-") if i % 2 == 0 else move(below, "z+")
        column = call(stack_kernel, (full, hi - lo), spot, here, below, above, far)
        own = dot(left_basis, column, (0, 0)).astype(BF)
        own_x = move(own, "xp")
        part = dot(left_part, column, (0, 0)).astype(BF)
        part = move(part, "yp")
        part_x = move(part, "xp")
        ours = jnp.concatenate([own, part, own_x, part_x], 1)
        term = dot(ours, right[2 * i], (1, 1))
        rotated = term if rotated is None else rotated + term
        theirs = move(ours, "co")
        rotated = rotated + dot(theirs, right[2 * i + 1], (1, 1))

    first_full = 0.8 * first_moment.astype(F32) + 0.2 * rotated
    second_full = 0.9 * second_moment.astype(F32) + 0.1 * rotated * rotated
    damping = jnp.minimum(left_eig[:, None] * right_eig[None, :], 1.0)
    direction = (first_full / jnp.sqrt(second_full + damping)).astype(BF)

    done = []
    for i, (lo, hi) in enumerate(spans):
        w = hi - lo
        sent = dot(direction, right[2 * i + 1], (1, 0)).astype(BF)
        sent = move(sent, "co")
        sums = dot(direction, right[2 * i], (1, 0)) + sent.astype(F32)
        if i == 0:
            away = move(sums[:, 3 * w :].astype(BF), "xp")
            near = move(sums[:, 2 * w : 3 * w].astype(BF), "xp")
        else:
            both = move(sums[:, 2 * w :].astype(BF), "xp")
            near, away = both[:, :w], both[:, w:]
        part = (sums[:, w : 2 * w] + away.astype(F32)).astype(BF)
        part = move(part, "yp")
        own = (sums[:, :w] + near.astype(F32)).astype(BF)
        product = dot(left_basis, own, (1, 0)) + dot(left_part, part, (1, 0))
        first, last = (1, 3) if i % 2 == 0 else (3, 1)
        shape = (2 * rows, w)
        p_far, p_last, p_first, p_here = call(
            functools.partial(split_kernel, (2, last, first, 0)),
            [jax.ShapeDtypeStruct(shape, t) for t in (BF, BF, F32, F32)],
            spot,
            product,
        )
        ways = ("z+", "z-") if i % 2 == 0 else ("z-", "z+")
        p_far = move(p_far, ways[0])
        p_first = (p_first + p_far.astype(F32)).astype(BF)
        last = move(p_last, ways[1])
        first = move(p_first, ways[0])
        cell = rows // 16

        def packed(kernel, count, shape, *operands):
            outs = [jax.ShapeDtypeStruct(shape + (cell, w), BF)] * count
            return call(kernel, outs, spot, *operands)

        stay, go = packed(sum_kernel, 2, (16,), p_here, first, last)
        come = move(go, "co")
        by_y = packed(pack_y_kernel, 4, (2, 4), stay, come)
        by_y = [by_y[0], move(by_y[1], "y-"), move(by_y[2], "y2"), move(by_y[3], "y+")]
        by_x = packed(pack_x_kernel, 4, (4, 2), *by_y)
        done += [by_x[0], move(by_x[1], "x-"), move(by_x[2], "x2"), move(by_x[3], "x+")]
    update = call(
        functools.partial(place_kernel, CUTS), (rows // 16, cols * 16), spot, *done
    )
    return (first_full.astype(BF), second_full.astype(BF), update)


def solution(mesh):
    placed = (
        P("row", "col"),
        P("row", "col"),
        P("row", "col"),
        P(None, "row"),
        P("col", None),
        P("row"),
        P("col"),
    )
    return jax.shard_map(
        step,
        mesh=mesh,
        in_specs=placed,
        out_specs=(P("row", "col"), P("row", "col"), P(("row", "col"), None)),
        check_vma=False,
    )
```
